32 devices in a mesh: dp: 16 (over z, x, core), tensor: 2 (over y).
Axes of the slice: x: 2, y: 2, z: 4, core: 2. Of those that a mesh axis runs over, the one named last changes fastest.
Arguments:
- tokens: bfloat16 [2048, 1024], P(('dp', 'tensor')), may hold values from -6 to 6
- out_grad: bfloat16 [2048, 1024], P(('dp', 'tensor')), may hold values from -6 to 6
- lengths: int32 [16, 6], P('dp'), may hold values from 1 to 64, 128 in all within a row
- routes: int32 [2048, 8], P('dp'), may hold values from 0 to 31, all different within a row; in each aligned block of 128 rows (0 to 127, 128 to 255, ...) at most 48 rows name the same one
- attn_gain: float32 [1024], replicated, may hold values from 0.25 to 1.75
- w_query: bfloat16 [1024, 1024], P('dp', 'tensor'), may hold values from -0.1875 to 0.1875
- w_key: bfloat16 [1024, 512], P('dp', 'tensor'), may hold values from -0.1875 to 0.1875
- w_value: bfloat16 [1024, 512], P('dp', 'tensor'), may hold values from -0.1875 to 0.1875
- w_out: bfloat16 [1024, 1024], P('dp', 'tensor'), may hold values from -3 to 3
- ffn_gain: float32 [1024], replicated, may hold values from 0.25 to 1.75
- w_router: float32 [1024, 32], replicated, may hold values from -0.1875 to 0.1875
- w_gate: bfloat16 [32, 1024, 512], P(None, 'dp', 'tensor'), may hold values from -0.1875 to 0.1875
- w_up: bfloat16 [32, 1024, 512], P(None, 'dp', 'tensor'), may hold values from -0.1875 to 0.1875
- w_down: bfloat16 [32, 1024, 512], P(None, 'dp', 'tensor'), may hold values from -3 to 3
Outputs:
- block_out: bfloat16 [2048, 1024], P(('dp', 'tensor'))
- tokens_grad: float32 [2048, 1024], P(('dp', 'tensor'))
- attn_gain_grad: float32 [1024], replicated
- w_query_grad: float32 [1024, 1024], P('dp', 'tensor')
- w_key_grad: float32 [1024, 512], P('dp', 'tensor')
- w_value_grad: float32 [1024, 512], P('dp', 'tensor')
- w_out_grad: float32 [1024, 1024], P('dp', 'tensor')
- ffn_gain_grad: float32 [1024], replicated
- w_router_grad: float32 [1024, 32], replicated
- w_gate_grad: float32 [32, 1024, 512], P(None, 'dp', 'tensor')
- w_up_grad: float32 [32, 1024, 512], P(None, 'dp', 'tensor')
- w_down_grad: float32 [32, 1024, 512], P(None, 'dp', 'tensor')
The draws below stay inside these ranges and needn't reach their ends.
Inputs may be any that keep to these rules, and one draw needn't show every extreme that they name: Each group's lengths sum to 128. `routes`: each row names 8 different experts; within the rows of one dp group no expert is named more than 48 times.
All inputs are finite; a program needn't handle non-finite values.
Results may differ from the reference program's by a relative error of at most 0.012.
The reference program's roundings to bfloat16 on the way count: a program that leaves them out, or rounds other values in their place, can miss the bound.
Values may be sent and summed in bfloat16 or wider, within the bound.
A program may use at most 128 MiB of HBM per device.

```python
import math
import jax
import jax.numpy as jnp
import numpy as np
from jax import lax

D = 1024
HEADS = 16
KV_HEADS = 8
EXPERTS = 32
FFE = 512
TOPK = 8
TOK_DEV = 128
SEQS = 6
HEAD_DIM = 64
MAXLEN = 64
MOST = 48
GROUPS = 16
TOKENS = 2048
N_TENSOR = 2


def levels(own_key, extent, cuts, least, largest):
    factor_of, own = 1.0, jax.random.fold_in(own_key, 6)
    for axis_at, parts in cuts:
        steps = jnp.exp(jax.random.uniform(jax.random.fold_in(own, axis_at), (parts,), jnp.float32, least / len(cuts), largest / len(cuts)))
        factor_of = factor_of * jnp.repeat(steps, extent[axis_at] // parts).reshape([-1 if axis == axis_at else 1 for axis in range(len(extent))])
    return factor_of


def length_profile(amount, total, most, slope):
    portions = [(1 << 20) // math.isqrt(rank ** slope) + 1 for rank in range(2, amount + 1)]
    spare, counts = total - most - (amount - 1), [1] * (amount - 1)
    while spare > 0:
        movable = [i for i in range(amount - 1) if counts[i] < most]
        pool, left = sum([portions[i] for i in movable]), spare
        for i in movable:
            more = min(most - counts[i], max(1, left * portions[i] // pool), spare)
            counts[i] = counts[i] + more
            spare = spare - more
    return np.array([most] + counts)


def uneven_parts(rng, count, total, bound, slope):
    if count == 2:
        one = jax.random.randint(rng, (), max(1, total - bound), min(bound, total - 1) + 1)
        return jnp.stack([one, total - one])
    sizes = jnp.asarray(length_profile(count, total, bound, slope), jnp.int32)
    couples = (count - 1) // 2
    source_of, sink = sizes[1:1 + 2 * couples:2], sizes[2:2 + 2 * couples:2]
    margin = jnp.minimum(source_of - 1, bound - sink)
    moved = jax.random.randint(jax.random.fold_in(rng, 1), (couples,), 0, 1 << 20) % (margin + 1)
    sizes = sizes.at[1:1 + 2 * couples:2].set(source_of - moved).at[2:2 + 2 * couples:2].set(sink + moved)
    return sizes[jax.random.permutation(jax.random.fold_in(rng, 2), count)]


def shared_out(key, own, number, rows, amount, top, most, slope):
    ranking = jax.random.permutation(key, amount)
    heavy_load, common = load_shares(amount, rows * top, most, slope, True), load_shares(amount, rows * top, most, slope, False)
    places = jnp.arange(amount)

    def named(tallies, turn):
        used = int((tallies > 0).sum())
        fixed = max(1, used // 4)
        passed = fixed + (places - fixed + turn * (used - fixed)) % max(1, amount - fixed)
        return jnp.zeros((amount,), jnp.int32).at[ranking[jnp.where(places < fixed, places, passed)]].set(jnp.asarray(tallies, jnp.int32))

    tallies = jnp.where(number % 4 == 0, named(heavy_load, number // 4), named(common, number - number // 4 - 1))
    mixed = jax.random.permutation(jax.random.fold_in(own, 3), amount)
    donor, sink = mixed[0:amount // 2 * 2:2], mixed[1:amount // 2 * 2:2]
    slack = jnp.minimum(tallies[donor] - 1, most - tallies[sink]) // 2
    slack = jnp.where((donor == ranking[0]) | (sink == ranking[0]) | (tallies[sink] == 0), 0, jnp.maximum(slack, 0))
    passed = jax.random.randint(jax.random.fold_in(own, 4), (amount // 2,), 0, 1 << 20) % (slack + 1)
    tallies = tallies.at[donor].add(-passed).at[sink].add(passed)
    labels = jnp.searchsorted(jnp.cumsum(tallies), jnp.arange(rows * top), side="right").astype(jnp.int32)
    grid = labels.reshape(top, rows).T
    grid = grid[jax.random.permutation(jax.random.fold_in(own, 1), rows)]
    turn = jax.random.randint(jax.random.fold_in(own, 2), (rows, 1), 0, top)
    return jnp.take_along_axis(grid, (jnp.arange(top)[None, :] + turn) % top, axis=1)


def load_shares(count, total, most, lean, full):
    portions = [(1 << 20) // math.isqrt(rank ** lean) + 1 for rank in range(1, count + 1)]
    largest = most if full else min(most, max(-(-total // count), total * portions[0] // sum(portions)))
    least = 1 if total - largest >= count - 1 else 0
    counts, rest = [largest] + [least] * (count - 1), total - largest - least * (count - 1)
    while rest > 0:
        movable = [i for i in range(1, count) if counts[i] < largest] or [i for i in range(1, count) if counts[i] < most]
        pool, left = sum([portions[i] for i in movable]), rest
        for i in movable:
            more = min(most - counts[i], max(1, left * portions[i] // pool), rest)
            counts[i] = counts[i] + more
            rest = rest - more
    return np.array(counts)


def scatter_about(stream_key, extent, scale, reach, split=(), kind=jnp.bfloat16):
    result = scale * jax.random.normal(stream_key, extent, jnp.float32)
    if split:
        result = result * levels(stream_key, extent, split, -0.22, 0.18)
    return jnp.clip(result, -reach, reach).astype(kind)


def setup_inputs(seed: int = 0) -> dict:
    key_list = jax.random.split(jax.random.key(seed), 15)
    tokens = scatter_about(key_list[0], (TOKENS, D), 1.0, 6.0, ((0, 32),))
    out_grad = scatter_about(key_list[1], (TOKENS, D), 1.0, 6.0, ((0, 32),))
    lengths = jax.vmap(lambda own: uneven_parts(own, SEQS, TOK_DEV, MAXLEN, 2))(jax.random.split(key_list[2], GROUPS)).reshape((GROUPS, SEQS)).astype(jnp.int32)
    routes_keys = jax.random.split(jax.random.fold_in(key_list[3], 1), TOKENS // TOK_DEV)
    routes_turns = jax.random.permutation(jax.random.fold_in(key_list[3], 3), TOKENS // TOK_DEV)
    routes = jax.vmap(lambda own, number: shared_out(jax.random.fold_in(key_list[3], 2), own, number, TOK_DEV, EXPERTS, TOPK, MOST, 2))(routes_keys, routes_turns).reshape((TOKENS, TOPK))
    attn_gain = jnp.clip(1.0 + 0.15 * jax.random.normal(key_list[4], (D,), jnp.float32), 0.25, 1.75)
    w_query = scatter_about(key_list[5], (D, HEADS * HEAD_DIM), D ** -0.5, 0.1875, ((0, 16), (1, 2)))
    w_key = scatter_about(key_list[6], (D, KV_HEADS * HEAD_DIM), D ** -0.5, 0.1875, ((0, 16), (1, 2)))
    w_value = scatter_about(key_list[7], (D, KV_HEADS * HEAD_DIM), D ** -0.5, 0.1875, ((0, 16), (1, 2)))
    w_out = scatter_about(key_list[8], (D, HEADS * HEAD_DIM), 4 ** -0.5, 3.0, ((0, 16), (1, 2)))
    ffn_gain = jnp.clip(1.0 + 0.15 * jax.random.normal(key_list[9], (D,), jnp.float32), 0.25, 1.75)
    w_router = scatter_about(key_list[10], (D, EXPERTS), D ** -0.5, 0.1875, (), jnp.float32)
    w_gate = scatter_about(key_list[11], (EXPERTS, D, FFE), D ** -0.5, 0.1875, ((1, 16), (2, 2)))
    w_up = scatter_about(key_list[12], (EXPERTS, D, FFE), D ** -0.5, 0.1875, ((1, 16), (2, 2)))
    w_down = scatter_about(key_list[13], (EXPERTS, D, FFE), 0.5, 3.0, ((1, 16), (2, 2)))
    return dict(tokens=tokens, out_grad=out_grad, lengths=lengths, routes=routes, attn_gain=attn_gain, w_query=w_query, w_key=w_key, w_value=w_value, w_out=w_out, ffn_gain=ffn_gain, w_router=w_router, w_gate=w_gate, w_up=w_up, w_down=w_down)


eps_norm = 1e-06
residual_scale = 0.22
score_scale = 0.015625
rope_base = 10000.0
masked_score = -1e+30

def to_bf16(array_in):
    return lax.optimization_barrier(array_in.astype(jnp.bfloat16))

def norm_forward(row_block, gain_vec):
    rscale = lax.rsqrt(lax.optimization_barrier(jnp.mean(row_block * row_block, axis=1, keepdims=True)) + eps_norm)
    unit_rows = row_block * rscale
    return (unit_rows, rscale, (unit_rows * gain_vec).astype(jnp.bfloat16))

def norm_backward(gradient, unit_rows, rscale, gain_vec):
    unit_grad = gradient * gain_vec
    back_rows = rscale * (unit_grad - unit_rows * lax.optimization_barrier(jnp.mean(unit_grad * unit_rows, axis=1, keepdims=True)))
    return (back_rows, lax.optimization_barrier(jnp.sum(gradient * unit_rows, axis=0)))

def seq_layout(seq_lengths, row_count):
    seq_ends = jnp.cumsum(seq_lengths).astype(jnp.int32)
    starts = seq_ends - seq_lengths
    places = jnp.arange(row_count, dtype=jnp.int32)
    segment = lax.optimization_barrier(jnp.sum((places[:, None] >= seq_ends[None, :]).astype(jnp.int32), axis=1))
    member = segment[:, None] == jnp.arange(seq_lengths.shape[0], dtype=jnp.int32)[None, :]
    offset = lax.optimization_barrier(jnp.sum(jnp.where(member, starts[None, :], 0), axis=1)).astype(jnp.int32)
    allowed = (segment[:, None] == segment[None, :]) & (places[None, :] <= places[:, None])
    return (places - offset, allowed)

def rope_tables(position, head_width):
    frequency = rope_base ** (-(jnp.arange(head_width // 2, dtype=jnp.float32) * 2.0) / head_width)
    angles = position.astype(jnp.float32)[:, None] * frequency[None, :]
    cosine = jnp.concatenate([jnp.cos(angles), jnp.cos(angles)], axis=1)[:, None, :]
    sine_table = jnp.concatenate([jnp.sin(angles), jnp.sin(angles)], axis=1)[:, None, :]
    return (cosine, sine_table)

def rotate(vectors, cosine, sine_table):
    half_width = vectors.shape[-1] // 2
    first_half = vectors[..., :half_width]
    second_half = vectors[..., half_width:]
    return vectors * cosine + jnp.concatenate([-second_half, first_half], axis=-1) * sine_table

def unrotate(gradient, cosine, sine_table):
    half_width = gradient.shape[-1] // 2
    first_half = gradient[..., :half_width]
    second_half = gradient[..., half_width:]
    return gradient * cosine + jnp.concatenate([second_half, -first_half], axis=-1) * sine_table

def score_block(query_heads, key_heads, allowed):
    row_count, head_count, head_width = query_heads.shape
    kv_count = key_heads.shape[1]
    grouped = query_heads.astype(jnp.float32).reshape(row_count, kv_count, head_count // kv_count, head_width)
    scores = jnp.einsum('igrd,jgd->grij', grouped, key_heads.astype(jnp.float32)) * score_scale
    return (grouped, jnp.where(allowed[None, None], scores, masked_score))

def attend(query_heads, key_heads, value_heads, allowed):
    row_count, head_count, head_width = query_heads.shape
    grouped, scores = score_block(query_heads, key_heads, allowed)
    row_max = lax.optimization_barrier(jnp.max(scores, axis=-1, keepdims=True))
    log_total = row_max + jnp.log(lax.optimization_barrier(jnp.sum(jnp.exp(scores - row_max), axis=-1, keepdims=True)))
    prob_bf = to_bf16(jnp.exp(scores - log_total)).astype(jnp.float32)
    mixed_out = jnp.einsum('grij,jgd->igrd', prob_bf, value_heads.astype(jnp.float32))
    return (mixed_out.reshape(row_count, head_count * head_width).astype(jnp.bfloat16), log_total)

def attend_back(query_heads, key_heads, value_heads, allowed, log_total, mixed_grad):
    row_count, head_count, head_width = query_heads.shape
    kv_count = key_heads.shape[1]
    grouped, scores = score_block(query_heads, key_heads, allowed)
    prob_full = jnp.exp(scores - log_total)
    grad_heads = mixed_grad.astype(jnp.float32).reshape(row_count, kv_count, head_count // kv_count, head_width)
    dprobs = jnp.einsum('igrd,jgd->grij', grad_heads, value_heads.astype(jnp.float32))
    row_delta = lax.optimization_barrier(jnp.sum(prob_full * dprobs, axis=-1, keepdims=True))
    dscores = to_bf16(prob_full * (dprobs - row_delta)).astype(jnp.float32)
    dquery = jnp.einsum('grij,jgd->igrd', dscores, key_heads.astype(jnp.float32)) * score_scale
    key_grad = jnp.einsum('grij,igrd->jgd', dscores, grouped) * score_scale
    prob_bf = to_bf16(prob_full).astype(jnp.float32)
    dvalues = jnp.einsum('grij,igrd->jgd', prob_bf, grad_heads)
    return (dquery.reshape(row_count, head_count, head_width), key_grad, dvalues)

def group_pass(params, x_rows, grad_rows, seq_lengths, route_ids):
    attn_gain, w_query, w_key, w_value, w_out, ffn_gain, w_router, gate_full, up_full, down_full = params
    row_count = x_rows.shape[0]
    half_ff = FFE // N_TENSOR
    tokens_f32 = x_rows.astype(jnp.float32)
    position, allowed = seq_layout(seq_lengths, row_count)
    cosine, sine_table = rope_tables(position, HEAD_DIM)
    unit_first, scale_first, normed_first = norm_forward(tokens_f32, attn_gain)
    query_heads = rotate(jnp.dot(normed_first, w_query, preferred_element_type=jnp.float32).reshape(row_count, HEADS, HEAD_DIM), cosine, sine_table).astype(jnp.bfloat16)
    key_heads = rotate(jnp.dot(normed_first, w_key, preferred_element_type=jnp.float32).reshape(row_count, KV_HEADS, HEAD_DIM), cosine, sine_table).astype(jnp.bfloat16)
    value_heads = jnp.dot(normed_first, w_value, preferred_element_type=jnp.float32).astype(jnp.bfloat16).reshape(row_count, KV_HEADS, HEAD_DIM)
    mixed_out, log_total = attend(query_heads, key_heads, value_heads, allowed)
    hidden = tokens_f32 + residual_scale * jnp.dot(mixed_out, w_out.T, preferred_element_type=jnp.float32)
    unit_second, scale_second, normed_second = norm_forward(hidden, ffn_gain)
    expert_ids = jnp.arange(EXPERTS, dtype=jnp.int32)
    picked = route_ids[:, :, None] == expert_ids[None, None, :]
    logits = jnp.dot(normed_second.astype(jnp.float32), w_router, precision=lax.Precision.HIGHEST)
    chosen = lax.optimization_barrier(jnp.sum(jnp.where(picked, logits[:, None, :], 0.0), axis=2))
    gate_probs = jax.nn.softmax(chosen, axis=1)
    flat_ids = route_ids.reshape(-1)
    onehot = (flat_ids[:, None] == expert_ids[None, :]).astype(jnp.int32)
    ordinal = lax.optimization_barrier(jnp.sum((jnp.cumsum(onehot, axis=0) - 1) * onehot, axis=1))
    slot_index = (flat_ids * MOST + ordinal).astype(jnp.int32)
    token_of = jnp.arange(row_count * TOPK, dtype=jnp.int32) // TOPK
    rows_in = jnp.zeros((EXPERTS * MOST, D), jnp.bfloat16).at[slot_index].set(normed_second[token_of])
    rows_in = rows_in.reshape(EXPERTS, MOST, D).astype(jnp.float32)
    gate_pre = jnp.einsum('ecd,edf->ecf', rows_in, gate_full)
    up_pre = jnp.einsum('ecd,edf->ecf', rows_in, up_full)
    sigmoid_gate = jax.nn.sigmoid(gate_pre)
    activated = gate_pre * sigmoid_gate
    inner_act = to_bf16(activated * up_pre).astype(jnp.float32)
    down_split = down_full.reshape(EXPERTS, D, N_TENSOR, half_ff)
    out_split = to_bf16(jnp.einsum('ecnf,ednf->necd', inner_act.reshape(EXPERTS, MOST, N_TENSOR, half_ff), down_split)).astype(jnp.float32)
    routed = out_split.reshape(N_TENSOR, EXPERTS * MOST, D)[:, slot_index]
    routed_sum = lax.optimization_barrier(jnp.sum(routed, axis=0)).reshape(row_count, TOPK, D)
    moe_out = lax.optimization_barrier(jnp.sum(gate_probs[:, :, None] * routed_sum, axis=1))
    block_rows = (hidden + residual_scale * moe_out).astype(jnp.bfloat16)
    out_f32 = grad_rows.astype(jnp.float32)
    moe_grad = to_bf16(residual_scale * out_f32).astype(jnp.float32)
    gate_grad = lax.optimization_barrier(jnp.sum(moe_grad[:, None, :] * routed_sum, axis=2))
    route_grad = to_bf16(gate_probs[:, :, None] * moe_grad[:, None, :]).astype(jnp.float32)
    grad_in = jnp.zeros((EXPERTS * MOST, D), jnp.float32).at[slot_index].set(route_grad.reshape(row_count * TOPK, D))
    grad_in = grad_in.reshape(EXPERTS, MOST, D)
    inner_grad = jnp.einsum('ecd,edf->ecf', grad_in, down_full)
    gate_pre_grad = to_bf16(inner_grad * up_pre * sigmoid_gate * (1.0 + gate_pre * (1.0 - sigmoid_gate))).astype(jnp.float32)
    up_pre_grad = to_bf16(inner_grad * activated).astype(jnp.float32)
    gate_split = gate_full.reshape(EXPERTS, D, N_TENSOR, half_ff)
    up_split = up_full.reshape(EXPERTS, D, N_TENSOR, half_ff)
    back_split = jnp.einsum('ecnf,ednf->necd', gate_pre_grad.reshape(EXPERTS, MOST, N_TENSOR, half_ff), gate_split)
    back_split = back_split + jnp.einsum('ecnf,ednf->necd', up_pre_grad.reshape(EXPERTS, MOST, N_TENSOR, half_ff), up_split)
    back_split = to_bf16(back_split).astype(jnp.float32)
    routed_back = back_split.reshape(N_TENSOR, EXPERTS * MOST, D)[:, slot_index].reshape(N_TENSOR, row_count, TOPK, D)
    expert_back = lax.optimization_barrier(jnp.sum(routed_back, axis=(0, 2)))
    w_gate_grad = jnp.einsum('ecd,ecf->edf', rows_in, gate_pre_grad)
    w_up_grad = jnp.einsum('ecd,ecf->edf', rows_in, up_pre_grad)
    w_down_grad = jnp.einsum('ecd,ecf->edf', grad_in, inner_act)
    chosen_grad = gate_probs * (gate_grad - lax.optimization_barrier(jnp.sum(gate_probs * gate_grad, axis=1, keepdims=True)))
    logits_grad = lax.optimization_barrier(jnp.sum(jnp.where(picked, chosen_grad[:, :, None], 0.0), axis=1))
    second_grad = expert_back + jnp.dot(logits_grad, w_router.T, precision=lax.Precision.HIGHEST)
    w_router_grad = jnp.dot(normed_second.astype(jnp.float32).T, logits_grad, precision=lax.Precision.HIGHEST)
    hidden_back, ffn_gain_grad = norm_backward(second_grad, unit_second, scale_second, ffn_gain)
    hidden_grad = out_f32 + hidden_back
    attn_grad = (residual_scale * hidden_grad).astype(jnp.bfloat16)
    mixed_grad = jnp.dot(attn_grad, w_out, preferred_element_type=jnp.float32).astype(jnp.bfloat16)
    w_out_grad = jnp.dot(attn_grad.T, mixed_out, preferred_element_type=jnp.float32)
    dquery, key_grad, dvalues = attend_back(query_heads, key_heads, value_heads, allowed, log_total, mixed_grad)
    query_grad = unrotate(dquery, cosine, sine_table).astype(jnp.bfloat16).reshape(row_count, HEADS * HEAD_DIM)
    keys_grad = unrotate(key_grad, cosine, sine_table).astype(jnp.bfloat16).reshape(row_count, KV_HEADS * HEAD_DIM)
    value_grad = dvalues.astype(jnp.bfloat16).reshape(row_count, KV_HEADS * HEAD_DIM)
    w_query_grad = jnp.dot(normed_first.T, query_grad, preferred_element_type=jnp.float32)
    w_key_grad = jnp.dot(normed_first.T, keys_grad, preferred_element_type=jnp.float32)
    w_value_grad = jnp.dot(normed_first.T, value_grad, preferred_element_type=jnp.float32)
    first_grad = jnp.dot(query_grad, w_query.T, preferred_element_type=jnp.float32)
    first_grad = first_grad + jnp.dot(keys_grad, w_key.T, preferred_element_type=jnp.float32)
    first_grad = first_grad + jnp.dot(value_grad, w_value.T, preferred_element_type=jnp.float32)
    tokens_back, attn_gain_grad = norm_backward(first_grad, unit_first, scale_first, attn_gain)
    tokens_grad = hidden_grad + tokens_back
    grads = (attn_gain_grad, w_query_grad, w_key_grad, w_value_grad, w_out_grad, ffn_gain_grad, w_router_grad, w_gate_grad, w_up_grad, w_down_grad)
    return (block_rows, tokens_grad, grads)

def reference(tokens, out_grad, lengths, routes, attn_gain, w_query, w_key, w_value, w_out, ffn_gain, w_router, w_gate, w_up, w_down):
    params = (attn_gain, w_query, w_key, w_value, w_out, ffn_gain, w_router, w_gate.astype(jnp.float32), w_up.astype(jnp.float32), w_down.astype(jnp.float32))
    group_count = lengths.shape[0]
    row_count = tokens.shape[0] // group_count
    inputs = (tokens.reshape(group_count, row_count, D), out_grad.reshape(group_count, row_count, D), lengths, routes.reshape(group_count, row_count, TOPK))
    zero_totals = (jnp.zeros((D,), jnp.float32), jnp.zeros(w_query.shape, jnp.float32), jnp.zeros(w_key.shape, jnp.float32), jnp.zeros(w_value.shape, jnp.float32), jnp.zeros(w_out.shape, jnp.float32), jnp.zeros((D,), jnp.float32), jnp.zeros(w_router.shape, jnp.float32), jnp.zeros(w_gate.shape, jnp.float32), jnp.zeros(w_up.shape, jnp.float32), jnp.zeros(w_down.shape, jnp.float32))

    def group_step(totals_acc, group_item):
        block_rows, tokens_grad, grads = group_pass(params, group_item[0], group_item[1], group_item[2], group_item[3])
        return (jax.tree.map(jnp.add, totals_acc, grads), (block_rows, tokens_grad))
    totals, (block_all, grad_all) = lax.scan(group_step, zero_totals, inputs)
    return (block_all.reshape(-1, D), grad_all.reshape(-1, D), totals[0], totals[1], totals[2], totals[3], totals[4], totals[5], totals[6], totals[7], totals[8], totals[9])
```

```python
import jax
import jax.numpy as jnp
from jax import lax
from jax.sharding import PartitionSpec as P

EXPERTS = 32
TOPK = 8
HEAD_DIM = 64


eps_norm = 1e-06
residual_scale = 0.22
score_scale = 0.015625
rope_base = 10000.0
masked_score = -1e30


def norm_forward(row_block, gain_vec):
    rscale = lax.rsqrt(jnp.mean(row_block * row_block, axis=1, keepdims=True) + eps_norm)
    unit_rows = row_block * rscale
    return (unit_rows, rscale, (unit_rows * gain_vec).astype(jnp.bfloat16))


def norm_backward(gradient, unit_rows, rscale, gain_vec):
    unit_grad = gradient * gain_vec
    back_rows = rscale * (
        unit_grad - unit_rows * jnp.mean(unit_grad * unit_rows, axis=1, keepdims=True)
    )
    return (back_rows, jnp.sum(gradient * unit_rows, axis=0))


def seq_layout(seq_lengths, row_count):
    seq_ends = jnp.cumsum(seq_lengths)
    starts = seq_ends - seq_lengths
    places = jnp.arange(row_count, dtype=jnp.int32)
    segment = jnp.sum((places[:, None] >= seq_ends[None, :]).astype(jnp.int32), axis=1)
    member = segment[:, None] == jnp.arange(seq_lengths.shape[0], dtype=jnp.int32)[None, :]
    offset = jnp.sum(jnp.where(member, starts[None, :], 0), axis=1)
    allowed = (segment[:, None] == segment[None, :]) & (places[None, :] <= places[:, None])
    return (places - offset, allowed)


def rope_tables(position, head_width):
    frequency = rope_base ** (-(jnp.arange(head_width // 2, dtype=jnp.float32) * 2.0) / head_width)
    angles = position.astype(jnp.float32)[:, None] * frequency[None, :]
    cosine = jnp.concatenate([jnp.cos(angles), jnp.cos(angles)], axis=1)[:, None, :]
    sine_table = jnp.concatenate([jnp.sin(angles), jnp.sin(angles)], axis=1)[:, None, :]
    return (cosine, sine_table)


def rotate(vectors, cosine, sine_table):
    half_width = vectors.shape[-1] // 2
    first_half = vectors[..., :half_width]
    second_half = vectors[..., half_width:]
    return vectors * cosine + jnp.concatenate([-second_half, first_half], axis=-1) * sine_table


def unrotate(gradient, cosine, sine_table):
    half_width = gradient.shape[-1] // 2
    first_half = gradient[..., :half_width]
    second_half = gradient[..., half_width:]
    return gradient * cosine + jnp.concatenate([second_half, -first_half], axis=-1) * sine_table


def score_block(query_heads, key_heads, allowed):
    row_count, head_count, head_width = query_heads.shape
    kv_count = key_heads.shape[1]
    grouped = query_heads.reshape(row_count, kv_count, head_count // kv_count, head_width)
    scores = (
        jnp.einsum("igrd,jgd->grij", grouped, key_heads, preferred_element_type=jnp.float32)
        * score_scale
    )
    return (grouped, jnp.where(allowed[None, None], scores, masked_score))


def attend(query_heads, key_heads, value_heads, allowed):
    row_count, head_count, head_width = query_heads.shape
    grouped, scores = score_block(query_heads, key_heads, allowed)
    row_max = jnp.max(scores, axis=-1, keepdims=True)
    log_total = row_max + jnp.log(jnp.sum(jnp.exp(scores - row_max), axis=-1, keepdims=True))
    prob_bf = jnp.exp(scores - log_total).astype(jnp.bfloat16)
    mixed_out = jnp.einsum(
        "grij,jgd->igrd", prob_bf, value_heads, preferred_element_type=jnp.float32
    )
    return (mixed_out.reshape(row_count, head_count * head_width).astype(jnp.bfloat16), log_total)


def attend_back(query_heads, key_heads, value_heads, allowed, log_total, mixed_grad):
    row_count, head_count, head_width = query_heads.shape
    kv_count = key_heads.shape[1]
    grouped, scores = score_block(query_heads, key_heads, allowed)
    prob_full = jnp.exp(scores - log_total)
    grad_heads = mixed_grad.reshape(row_count, kv_count, head_count // kv_count, head_width)
    dprobs = jnp.einsum(
        "igrd,jgd->grij", grad_heads, value_heads, preferred_element_type=jnp.float32
    )
    row_delta = jnp.sum(prob_full * dprobs, axis=-1, keepdims=True)
    dscores = (prob_full * (dprobs - row_delta)).astype(jnp.bfloat16)
    dquery = (
        jnp.einsum("grij,jgd->igrd", dscores, key_heads, preferred_element_type=jnp.float32)
        * score_scale
    )
    key_grad = (
        jnp.einsum("grij,igrd->jgd", dscores, grouped, preferred_element_type=jnp.float32)
        * score_scale
    )
    dvalues = jnp.einsum(
        "grij,igrd->jgd",
        prob_full.astype(jnp.bfloat16),
        grad_heads,
        preferred_element_type=jnp.float32,
    )
    return (dquery.reshape(row_count, head_count, head_width), key_grad, dvalues)


def spread_rows(row_block):
    return lax.all_gather(row_block, "tensor", axis=0, tiled=True)


def narrow(partial_rows):
    if lax.axis_size("tensor") != 2:
        return lax.psum_scatter(partial_rows, "tensor", scatter_dimension=0, tiled=True)
    half = partial_rows.shape[0] // 2
    mine = lax.axis_index("tensor")
    away = lax.dynamic_slice_in_dim(partial_rows, (1 - mine) * half, half, 0)
    kept = lax.dynamic_slice_in_dim(partial_rows, mine * half, half, 0)
    return kept + lax.ppermute(away, "tensor", [(0, 1), (1, 0)])


def split_three(values):
    high = lax.reduce_precision(values, 8, 7)
    rest = values - high
    middle = lax.reduce_precision(rest, 8, 7)
    return [part.astype(jnp.bfloat16) for part in (high, middle, rest - middle)]


def dot_f32(left, right, dims):
    return lax.dot_general(left, right, (dims, ((), ())), preferred_element_type=jnp.float32)


def exact_dot(rows_bf, values, dims):
    width = values.shape[1]
    product = dot_f32(rows_bf, jnp.concatenate(split_three(values), axis=1), dims)
    return product[:, :width] + (product[:, width : 2 * width] + product[:, 2 * width :])


def gather_dp(rows, groups):
    return lax.all_gather(rows, "dp", axis=0, tiled=True, axis_index_groups=groups)


def scatter_dp(rows, groups):
    return lax.psum_scatter(
        rows, "dp", scatter_dimension=0, tiled=True, axis_index_groups=groups
    )


def gather_weights(packed):
    return lax.all_gather(packed, "dp", axis=0, tiled=True)


def scatter_weights(packed):
    return lax.psum_scatter(packed, "dp", scatter_dimension=0, tiled=True)


def local(
    tokens,
    out_grad,
    lengths,
    routes,
    attn_gain,
    w_query,
    w_key,
    w_value,
    w_out,
    ffn_gain,
    w_router,
    w_gate,
    w_up,
    w_down,
):
    local_rows = tokens.shape[0]
    row_count = routes.shape[0]
    model_width = tokens.shape[1]
    dp_count = lax.axis_size("dp")
    replicas = max(1, dp_count // EXPERTS)
    holders = max(1, EXPERTS // dp_count)
    clusters = EXPERTS // holders
    half_ff = w_gate.shape[2]
    heads_here = w_query.shape[1] // HEAD_DIM
    kv_here = w_key.shape[1] // HEAD_DIM
    own_row = lax.axis_index("tensor") * local_rows
    groups = (
        None
        if replicas == 1
        else [[r * clusters + c for c in range(clusters)] for r in range(replicas)]
    )
    q_cols, k_cols = w_query.shape[1], w_key.shape[1]
    cuts = (q_cols, q_cols + k_cols, q_cols + 2 * k_cols)
    packed_attn = gather_weights(jnp.concatenate([w_query, w_key, w_value, w_out], axis=1))
    full_qkv = packed_attn[:, : cuts[2]]
    full_out = packed_attn[:, cuts[2] :]

    def spread_out(weight):
        grouped = weight.reshape(clusters, holders, weight.shape[1], half_ff)
        return jnp.broadcast_to(grouped[None], (replicas,) + grouped.shape).reshape(
            dp_count, holders, weight.shape[1], half_ff
        )

    def fetch(weight):
        moved = lax.all_to_all(spread_out(weight), "dp", split_axis=0, concat_axis=2, tiled=True)
        return moved.reshape(holders, model_width, half_ff)

    local_gate, local_up, local_down = fetch(w_gate), fetch(w_up), fetch(w_down)
    tokens_f32 = tokens.astype(jnp.float32)
    out_f32 = out_grad.astype(jnp.float32)
    position, allowed = seq_layout(lengths[0], row_count)
    cosine, sine_table = rope_tables(position, HEAD_DIM)
    unit_first, scale_first, normed_first = norm_forward(tokens_f32, attn_gain)
    both = spread_rows(
        jnp.concatenate(
            [normed_first, (residual_scale * out_f32).astype(jnp.bfloat16)], axis=1
        )
    )
    wide_first = both[:, :model_width]
    tagged = jnp.concatenate(
        [
            both[:, model_width:],
            jnp.pad(routes.astype(jnp.bfloat16), ((0, 0), (0, 128 - TOPK))),
        ],
        axis=1,
    )
    tagged_all = gather_dp(tagged, groups)
    moe_all = tagged_all[:, :model_width]
    routes_all = tagged_all[:, model_width : model_width + TOPK].astype(jnp.int32)
    qkv = jnp.dot(wide_first, full_qkv, preferred_element_type=jnp.float32)
    query_heads = rotate(
        qkv[:, : cuts[0]].reshape(row_count, heads_here, HEAD_DIM), cosine, sine_table
    ).astype(jnp.bfloat16)
    key_heads = rotate(
        qkv[:, cuts[0] : cuts[1]].reshape(row_count, kv_here, HEAD_DIM), cosine, sine_table
    ).astype(jnp.bfloat16)
    value_heads = qkv[:, cuts[1] :].astype(jnp.bfloat16).reshape(row_count, kv_here, HEAD_DIM)
    mixed_out, log_total = attend(query_heads, key_heads, value_heads, allowed)
    hidden = tokens_f32 + residual_scale * narrow(dot_f32(mixed_out, full_out, ((1,), (1,))))
    unit_second, scale_second, normed_second = norm_forward(hidden, ffn_gain)
    rows_all = gather_dp(spread_rows(normed_second), groups)

    expert_ids = jnp.arange(EXPERTS, dtype=jnp.int32)

    def gate_of(rows_bf, row_routes):
        picked = row_routes[:, :, None] == expert_ids[None, None, :]
        logits = exact_dot(rows_bf, w_router, ((1,), (0,)))
        named = jnp.any(picked, axis=1)
        masked = jnp.where(named, logits, -jnp.inf)
        raised = jnp.exp(masked - jnp.max(masked, axis=1, keepdims=True))
        return picked, named, raised / jnp.sum(raised, axis=1, keepdims=True)

    _, named_all, gates_all = gate_of(rows_all, routes_all)
    first_expert = lax.axis_index("dp") % clusters * holders
    out_part = back_part = gate_slots = 0.0
    grads = []
    for h in range(holders):
        gate = lax.dynamic_slice_in_dim(gates_all, first_expert + h, 1, 1)
        here = lax.dynamic_slice_in_dim(named_all, first_expert + h, 1, 1)
        gate_pre = dot_f32(rows_all, local_gate[h], ((1,), (0,)))
        up_pre = dot_f32(rows_all, local_up[h], ((1,), (0,)))
        sigmoid_gate = jax.nn.sigmoid(gate_pre)
        activated = gate_pre * sigmoid_gate
        inner_act = (activated * up_pre).astype(jnp.bfloat16)
        produced = dot_f32(inner_act, local_down[h], ((1,), (1,))).astype(jnp.bfloat16)
        produced = produced.astype(jnp.float32)
        out_part = out_part + jnp.where(here, gate * produced, 0.0)
        moe_f32 = moe_all.astype(jnp.float32)
        gate_part = jnp.sum(moe_f32 * produced, axis=1, keepdims=True)
        gate_slots = gate_slots + jnp.where(routes_all == first_expert + h, gate_part, 0.0)
        route_grad = jnp.where(here, gate * moe_f32, 0.0).astype(jnp.bfloat16)
        inner_grad = dot_f32(route_grad, local_down[h], ((1,), (0,)))
        gate_pre_grad = (
            inner_grad * up_pre * sigmoid_gate * (1.0 + gate_pre * (1.0 - sigmoid_gate))
        ).astype(jnp.bfloat16)
        up_pre_grad = (inner_grad * activated).astype(jnp.bfloat16)
        back = dot_f32(gate_pre_grad, local_gate[h], ((1,), (1,))) + dot_f32(
            up_pre_grad, local_up[h], ((1,), (1,))
        )
        back_part = back_part + back.astype(jnp.bfloat16).astype(jnp.float32)
        grads.append(
            (
                dot_f32(rows_all, gate_pre_grad, ((0,), (0,))).astype(jnp.bfloat16),
                dot_f32(rows_all, up_pre_grad, ((0,), (0,))).astype(jnp.bfloat16),
                dot_f32(route_grad, inner_act, ((0,), (0,))).astype(jnp.bfloat16),
            )
        )
    slot_parts = split_three(gate_slots)
    pad = jnp.zeros((rows_all.shape[0], 128 - 3 * TOPK), jnp.bfloat16)
    back_home = scatter_dp(
        jnp.concatenate([back_part.astype(jnp.bfloat16)] + slot_parts + [pad], axis=1), groups
    ).astype(jnp.float32)
    out_home = scatter_dp(out_part.astype(jnp.bfloat16), groups).astype(jnp.float32)
    slots = back_home[:, model_width:]
    gate_half = slots[:, :TOPK] + slots[:, TOPK : 2 * TOPK] + slots[:, 2 * TOPK : 3 * TOPK]
    own_back = narrow(
        jnp.concatenate(
            [back_home[:, :model_width], jnp.pad(gate_half, ((0, 0), (0, 128 - TOPK)))], axis=1
        )
    )
    expert_back = own_back[:, :model_width]
    gate_grad = own_back[:, model_width : model_width + TOPK]
    block_rows = (hidden + residual_scale * narrow(out_home)).astype(jnp.bfloat16)

    def send_home(index):
        stacked = jnp.stack([grads[h][index] for h in range(holders)])
        moved = lax.all_to_all(stacked[None], "dp", split_axis=2, concat_axis=0, tiled=True)
        return jnp.sum(
            moved.astype(jnp.float32).reshape(
                replicas, clusters * holders, moved.shape[2], half_ff
            ),
            axis=0,
        )

    own_routes = lax.dynamic_slice_in_dim(routes, own_row, local_rows, 0)
    picked_own, _, gates_dense = gate_of(normed_second, own_routes)
    gates_own = jnp.sum(jnp.where(picked_own, gates_dense[:, None, :], 0.0), axis=2)
    chosen_grad = gates_own * (gate_grad - jnp.sum(gates_own * gate_grad, axis=1, keepdims=True))
    logits_grad = jnp.sum(jnp.where(picked_own, chosen_grad[:, :, None], 0.0), axis=1)
    second_grad = expert_back + jnp.dot(logits_grad, w_router.T, precision=lax.Precision.HIGHEST)
    if replicas == 1:
        logits_grad_all = lax.all_gather(logits_grad, ("dp", "tensor"), axis=0, tiled=True)
        router_total = exact_dot(rows_all, logits_grad_all, ((0,), (0,)))
    else:
        router_total = lax.psum(
            exact_dot(normed_second, logits_grad, ((0,), (0,))), ("dp", "tensor")
        )
    hidden_back, ffn_gain_grad = norm_backward(second_grad, unit_second, scale_second, ffn_gain)
    hidden_grad = out_f32 + hidden_back
    attn_grad = spread_rows((residual_scale * hidden_grad).astype(jnp.bfloat16))
    mixed_grad = jnp.dot(attn_grad, full_out, preferred_element_type=jnp.float32).astype(
        jnp.bfloat16
    )
    out_w_grad = dot_f32(attn_grad, mixed_out, ((0,), (0,)))
    dquery, key_grad, dvalues = attend_back(
        query_heads, key_heads, value_heads, allowed, log_total, mixed_grad
    )
    query_grad = (
        unrotate(dquery, cosine, sine_table)
        .astype(jnp.bfloat16)
        .reshape(row_count, heads_here * HEAD_DIM)
    )
    keys_grad = (
        unrotate(key_grad, cosine, sine_table)
        .astype(jnp.bfloat16)
        .reshape(row_count, kv_here * HEAD_DIM)
    )
    value_grad = dvalues.astype(jnp.bfloat16).reshape(row_count, kv_here * HEAD_DIM)
    qkv_grad = jnp.concatenate([query_grad, keys_grad, value_grad], axis=1)
    qkv_w_grad = dot_f32(wide_first, qkv_grad, ((0,), (0,)))
    packed_grad = scatter_weights(
        jnp.concatenate([qkv_w_grad, out_w_grad], axis=1).astype(jnp.bfloat16)
    ).astype(jnp.float32)
    first_grad = narrow(dot_f32(qkv_grad, full_qkv, ((1,), (1,))))
    tokens_back, attn_gain_grad = norm_backward(first_grad, unit_first, scale_first, attn_gain)
    tokens_grad = hidden_grad + tokens_back
    attn_gain_total, ffn_gain_total = lax.psum(
        (attn_gain_grad, ffn_gain_grad), ("dp", "tensor")
    )
    return (
        block_rows,
        tokens_grad,
        attn_gain_total,
        packed_grad[:, : cuts[0]],
        packed_grad[:, cuts[0] : cuts[1]],
        packed_grad[:, cuts[1] : cuts[2]],
        packed_grad[:, cuts[2] :],
        ffn_gain_total,
        router_total,
        send_home(0),
        send_home(1),
        send_home(2),
    )


def solution(mesh):
    placed = (
        P(("dp", "tensor"), None),
        P(("dp", "tensor"), None),
        P("dp", None),
        P("dp", None),
        P(),
        P("dp", "tensor"),
        P("dp", "tensor"),
        P("dp", "tensor"),
        P("dp", "tensor"),
        P(),
        P(),
        P(None, "dp", "tensor"),
        P(None, "dp", "tensor"),
        P(None, "dp", "tensor"),
    )
    return jax.shard_map(
        local,
        mesh=mesh,
        in_specs=placed,
        out_specs=(
            P(("dp", "tensor"), None),
            P(("dp", "tensor"), None),
            P(),
            P("dp", "tensor"),
            P("dp", "tensor"),
            P("dp", "tensor"),
            P("dp", "tensor"),
            P(),
            P(),
            P(None, "dp", "tensor"),
            P(None, "dp", "tensor"),
            P(None, "dp", "tensor"),
        ),
        check_vma=False,
    )
```

```python
import jax
import jax.numpy as jnp
from jax import lax
from jax.experimental import pallas as pl
from jax.experimental.pallas import tpu as pltpu
from jax.sharding import PartitionSpec as P

EXPERTS = 32
TOPK = 8
HEAD_DIM = 64


eps_norm = 1e-06
residual_scale = 0.22
score_scale = 0.015625
rope_base = 10000.0
masked_score = -1e30


def norm_forward(row_block, gain_vec):
    rscale = lax.rsqrt(jnp.mean(row_block * row_block, axis=1, keepdims=True) + eps_norm)
    unit_rows = row_block * rscale
    return (unit_rows, rscale, (unit_rows * gain_vec).astype(jnp.bfloat16))


def norm_backward(gradient, unit_rows, rscale, gain_vec):
    unit_grad = gradient * gain_vec
    back_rows = rscale * (
        unit_grad - unit_rows * jnp.mean(unit_grad * unit_rows, axis=1, keepdims=True)
    )
    return (back_rows, jnp.sum(gradient * unit_rows, axis=0))


def seq_layout(seq_lengths, row_count):
    seq_ends = jnp.cumsum(seq_lengths)
    starts = seq_ends - seq_lengths
    places = jnp.arange(row_count, dtype=jnp.int32)
    segment = jnp.sum((places[:, None] >= seq_ends[None, :]).astype(jnp.int32), axis=1)
    member = segment[:, None] == jnp.arange(seq_lengths.shape[0], dtype=jnp.int32)[None, :]
    offset = jnp.sum(jnp.where(member, starts[None, :], 0), axis=1)
    allowed = (segment[:, None] == segment[None, :]) & (places[None, :] <= places[:, None])
    return (places - offset, allowed)


def rope_tables(position, head_width):
    frequency = rope_base ** (-(jnp.arange(head_width // 2, dtype=jnp.float32) * 2.0) / head_width)
    angles = position.astype(jnp.float32)[:, None] * frequency[None, :]
    cosine = jnp.concatenate([jnp.cos(angles), jnp.cos(angles)], axis=1)[:, None, :]
    sine_table = jnp.concatenate([jnp.sin(angles), jnp.sin(angles)], axis=1)[:, None, :]
    return (cosine, sine_table)


def rotate(vectors, cosine, sine_table):
    half_width = vectors.shape[-1] // 2
    first_half = vectors[..., :half_width]
    second_half = vectors[..., half_width:]
    return vectors * cosine + jnp.concatenate([-second_half, first_half], axis=-1) * sine_table


def unrotate(gradient, cosine, sine_table):
    half_width = gradient.shape[-1] // 2
    first_half = gradient[..., :half_width]
    second_half = gradient[..., half_width:]
    return gradient * cosine + jnp.concatenate([second_half, -first_half], axis=-1) * sine_table


def score_block(query_heads, key_heads, allowed):
    row_count, head_count, head_width = query_heads.shape
    kv_count = key_heads.shape[1]
    grouped = query_heads.reshape(row_count, kv_count, head_count // kv_count, head_width)
    scores = (
        jnp.einsum("igrd,jgd->grij", grouped, key_heads, preferred_element_type=jnp.float32)
        * score_scale
    )
    return (grouped, jnp.where(allowed[None, None], scores, masked_score))


def attend(query_heads, key_heads, value_heads, allowed):
    row_count, head_count, head_width = query_heads.shape
    grouped, scores = score_block(query_heads, key_heads, allowed)
    row_max = jnp.max(scores, axis=-1, keepdims=True)
    log_total = row_max + jnp.log(jnp.sum(jnp.exp(scores - row_max), axis=-1, keepdims=True))
    prob_bf = jnp.exp(scores - log_total).astype(jnp.bfloat16)
    mixed_out = jnp.einsum(
        "grij,jgd->igrd", prob_bf, value_heads, preferred_element_type=jnp.float32
    )
    return (mixed_out.reshape(row_count, head_count * head_width).astype(jnp.bfloat16), log_total)


def attend_back(query_heads, key_heads, value_heads, allowed, log_total, mixed_grad):
    row_count, head_count, head_width = query_heads.shape
    kv_count = key_heads.shape[1]
    grouped, scores = score_block(query_heads, key_heads, allowed)
    prob_full = jnp.exp(scores - log_total)
    grad_heads = mixed_grad.reshape(row_count, kv_count, head_count // kv_count, head_width)
    dprobs = jnp.einsum(
        "igrd,jgd->grij", grad_heads, value_heads, preferred_element_type=jnp.float32
    )
    row_delta = jnp.sum(prob_full * dprobs, axis=-1, keepdims=True)
    dscores = (prob_full * (dprobs - row_delta)).astype(jnp.bfloat16)
    dquery = (
        jnp.einsum("grij,jgd->igrd", dscores, key_heads, preferred_element_type=jnp.float32)
        * score_scale
    )
    key_grad = (
        jnp.einsum("grij,igrd->jgd", dscores, grouped, preferred_element_type=jnp.float32)
        * score_scale
    )
    dvalues = jnp.einsum(
        "grij,igrd->jgd",
        prob_full.astype(jnp.bfloat16),
        grad_heads,
        preferred_element_type=jnp.float32,
    )
    return (dquery.reshape(row_count, head_count, head_width), key_grad, dvalues)


def spread_rows(row_block):
    return lax.all_gather(row_block, "tensor", axis=0, tiled=True)


def narrow(partial_rows):
    if lax.axis_size("tensor") != 2:
        return lax.psum_scatter(partial_rows, "tensor", scatter_dimension=0, tiled=True)
    half = partial_rows.shape[0] // 2
    mine = lax.axis_index("tensor")
    away = lax.dynamic_slice_in_dim(partial_rows, (1 - mine) * half, half, 0)
    kept = lax.dynamic_slice_in_dim(partial_rows, mine * half, half, 0)
    return kept + lax.ppermute(away, "tensor", [(0, 1), (1, 0)])


def split_three(values):
    high = lax.reduce_precision(values, 8, 7)
    rest = values - high
    middle = lax.reduce_precision(rest, 8, 7)
    return [part.astype(jnp.bfloat16) for part in (high, middle, rest - middle)]


def dot_f32(left, right, dims):
    return lax.dot_general(left, right, (dims, ((), ())), preferred_element_type=jnp.float32)


def exact_dot(rows_bf, values, dims):
    width = values.shape[1]
    product = dot_f32(rows_bf, jnp.concatenate(split_three(values), axis=1), dims)
    return product[:, :width] + (product[:, width : 2 * width] + product[:, 2 * width :])


def gather_dp(rows, groups):
    return lax.all_gather(rows, "dp", axis=0, tiled=True, axis_index_groups=groups)


def scatter_dp(rows, groups):
    return lax.psum_scatter(
        rows, "dp", scatter_dimension=0, tiled=True, axis_index_groups=groups
    )


def gather_weights(packed):
    return lax.all_gather(packed, "dp", axis=0, tiled=True)


def scatter_weights(packed):
    return lax.psum_scatter(packed, "dp", scatter_dimension=0, tiled=True)


def share_kernel(x_ref, o_ref, send_sem, recv_sem, own_sem):
    width = lax.axis_size("tensor")
    count = lax.axis_size("dp") * width
    me = lax.axis_index("dp") * width + lax.axis_index("tensor")
    barrier = pltpu.get_barrier_semaphore()

    def place(k):
        peer = lax.rem(me + k, count)
        return (lax.div(peer, width), lax.rem(peer, width))

    def greet(k, carry):
        pl.semaphore_signal(
            barrier, inc=1, device_id=place(k), device_id_type=pl.DeviceIdType.MESH
        )
        return carry

    def copy(k, slot):
        return pltpu.make_async_remote_copy(
            src_ref=x_ref,
            dst_ref=o_ref.at[slot],
            send_sem=send_sem.at[k],
            recv_sem=recv_sem.at[k],
            device_id=place(k),
            device_id_type=pl.DeviceIdType.MESH,
        )

    def start(k, carry):
        copy(k, me).start()
        return carry

    def finish(k, carry):
        copy(k, me).wait_send()
        copy(k, lax.rem(me - k + count, count)).wait_recv()
        return carry

    lax.fori_loop(1, count, greet, 0)
    pl.semaphore_wait(barrier, count - 1)
    own = pltpu.make_async_copy(x_ref, o_ref.at[me], own_sem)
    own.start()
    lax.fori_loop(1, count, start, 0)
    lax.fori_loop(1, count, finish, 0)
    own.wait()


def share(block):
    count = lax.axis_size("dp") * lax.axis_size("tensor")
    return pl.pallas_call(
        share_kernel,
        out_shape=jax.ShapeDtypeStruct((count,) + block.shape, block.dtype),
        in_specs=[pl.BlockSpec(memory_space=pltpu.VMEM)],
        out_specs=pl.BlockSpec(memory_space=pltpu.VMEM),
        scratch_shapes=[
            pltpu.SemaphoreType.DMA((count,)),
            pltpu.SemaphoreType.DMA((count,)),
            pltpu.SemaphoreType.DMA,
        ],
        compiler_params=pltpu.CompilerParams(collective_id=0, has_side_effects=True),
        name="share",
    )(block)


def local(
    tokens,
    out_grad,
    lengths,
    routes,
    attn_gain,
    w_query,
    w_key,
    w_value,
    w_out,
    ffn_gain,
    w_router,
    w_gate,
    w_up,
    w_down,
):
    local_rows = tokens.shape[0]
    row_count = routes.shape[0]
    model_width = tokens.shape[1]
    dp_count = lax.axis_size("dp")
    replicas = max(1, dp_count // EXPERTS)
    holders = max(1, EXPERTS // dp_count)
    clusters = EXPERTS // holders
    half_ff = w_gate.shape[2]
    heads_here = w_query.shape[1] // HEAD_DIM
    kv_here = w_key.shape[1] // HEAD_DIM
    own_row = lax.axis_index("tensor") * local_rows
    groups = (
        None
        if replicas == 1
        else [[r * clusters + c for c in range(clusters)] for r in range(replicas)]
    )
    q_cols, k_cols = w_query.shape[1], w_key.shape[1]
    cuts = (q_cols, q_cols + k_cols, q_cols + 2 * k_cols)
    packed_attn = gather_weights(jnp.concatenate([w_query, w_key, w_value, w_out], axis=1))
    full_qkv = packed_attn[:, : cuts[2]]
    full_out = packed_attn[:, cuts[2] :]

    def spread_out(weight):
        grouped = weight.reshape(clusters, holders, weight.shape[1], half_ff)
        return jnp.broadcast_to(grouped[None], (replicas,) + grouped.shape).reshape(
            dp_count, holders, weight.shape[1], half_ff
        )

    def fetch(weight):
        moved = lax.all_to_all(spread_out(weight), "dp", split_axis=0, concat_axis=2, tiled=True)
        return moved.reshape(holders, model_width, half_ff)

    local_gate, local_up, local_down = fetch(w_gate), fetch(w_up), fetch(w_down)
    tokens_f32 = tokens.astype(jnp.float32)
    out_f32 = out_grad.astype(jnp.float32)
    position, allowed = seq_layout(lengths[0], row_count)
    cosine, sine_table = rope_tables(position, HEAD_DIM)
    unit_first, scale_first, normed_first = norm_forward(tokens_f32, attn_gain)
    both = spread_rows(
        jnp.concatenate(
            [normed_first, (residual_scale * out_f32).astype(jnp.bfloat16)], axis=1
        )
    )
    wide_first = both[:, :model_width]
    tagged = jnp.concatenate(
        [
            both[:, model_width:],
            jnp.pad(routes.astype(jnp.bfloat16), ((0, 0), (0, 128 - TOPK))),
        ],
        axis=1,
    )
    tagged_all = gather_dp(tagged, groups)
    moe_all = tagged_all[:, :model_width]
    routes_all = tagged_all[:, model_width : model_width + TOPK].astype(jnp.int32)
    qkv = jnp.dot(wide_first, full_qkv, preferred_element_type=jnp.float32)
    query_heads = rotate(
        qkv[:, : cuts[0]].reshape(row_count, heads_here, HEAD_DIM), cosine, sine_table
    ).astype(jnp.bfloat16)
    key_heads = rotate(
        qkv[:, cuts[0] : cuts[1]].reshape(row_count, kv_here, HEAD_DIM), cosine, sine_table
    ).astype(jnp.bfloat16)
    value_heads = qkv[:, cuts[1] :].astype(jnp.bfloat16).reshape(row_count, kv_here, HEAD_DIM)
    mixed_out, log_total = attend(query_heads, key_heads, value_heads, allowed)
    hidden = tokens_f32 + residual_scale * narrow(dot_f32(mixed_out, full_out, ((1,), (1,))))
    unit_second, scale_second, normed_second = norm_forward(hidden, ffn_gain)
    rows_all = gather_dp(spread_rows(normed_second), groups)

    expert_ids = jnp.arange(EXPERTS, dtype=jnp.int32)

    def gate_of(rows_bf, row_routes):
        picked = row_routes[:, :, None] == expert_ids[None, None, :]
        logits = exact_dot(rows_bf, w_router, ((1,), (0,)))
        named = jnp.any(picked, axis=1)
        masked = jnp.where(named, logits, -jnp.inf)
        raised = jnp.exp(masked - jnp.max(masked, axis=1, keepdims=True))
        return picked, named, raised / jnp.sum(raised, axis=1, keepdims=True)

    _, named_all, gates_all = gate_of(rows_all, routes_all)
    first_expert = lax.axis_index("dp") % clusters * holders
    out_part = back_part = gate_slots = 0.0
    grads = []
    for h in range(holders):
        gate = lax.dynamic_slice_in_dim(gates_all, first_expert + h, 1, 1)
        here = lax.dynamic_slice_in_dim(named_all, first_expert + h, 1, 1)
        gate_pre = dot_f32(rows_all, local_gate[h], ((1,), (0,)))
        up_pre = dot_f32(rows_all, local_up[h], ((1,), (0,)))
        sigmoid_gate = jax.nn.sigmoid(gate_pre)
        activated = gate_pre * sigmoid_gate
        inner_act = (activated * up_pre).astype(jnp.bfloat16)
        produced = dot_f32(inner_act, local_down[h], ((1,), (1,))).astype(jnp.bfloat16)
        produced = produced.astype(jnp.float32)
        out_part = out_part + jnp.where(here, gate * produced, 0.0)
        moe_f32 = moe_all.astype(jnp.float32)
        gate_part = jnp.sum(moe_f32 * produced, axis=1, keepdims=True)
        gate_slots = gate_slots + jnp.where(routes_all == first_expert + h, gate_part, 0.0)
        route_grad = jnp.where(here, gate * moe_f32, 0.0).astype(jnp.bfloat16)
        inner_grad = dot_f32(route_grad, local_down[h], ((1,), (0,)))
        gate_pre_grad = (
            inner_grad * up_pre * sigmoid_gate * (1.0 + gate_pre * (1.0 - sigmoid_gate))
        ).astype(jnp.bfloat16)
        up_pre_grad = (inner_grad * activated).astype(jnp.bfloat16)
        back = dot_f32(gate_pre_grad, local_gate[h], ((1,), (1,))) + dot_f32(
            up_pre_grad, local_up[h], ((1,), (1,))
        )
        back_part = back_part + back.astype(jnp.bfloat16).astype(jnp.float32)
        grads.append(
            (
                dot_f32(rows_all, gate_pre_grad, ((0,), (0,))).astype(jnp.bfloat16),
                dot_f32(rows_all, up_pre_grad, ((0,), (0,))).astype(jnp.bfloat16),
                dot_f32(route_grad, inner_act, ((0,), (0,))).astype(jnp.bfloat16),
            )
        )
    slot_parts = split_three(gate_slots)
    pad = jnp.zeros((rows_all.shape[0], 128 - 3 * TOPK), jnp.bfloat16)
    home = scatter_dp(
        jnp.concatenate(
            [back_part.astype(jnp.bfloat16)] + slot_parts + [pad, out_part.astype(jnp.bfloat16)],
            axis=1,
        ),
        groups,
    ).astype(jnp.float32)
    back_home = home[:, : model_width + 128]
    out_home = home[:, model_width + 128 :]
    slots = back_home[:, model_width:]
    gate_half = slots[:, :TOPK] + slots[:, TOPK : 2 * TOPK] + slots[:, 2 * TOPK : 3 * TOPK]
    own_back = narrow(
        jnp.concatenate(
            [back_home[:, :model_width], jnp.pad(gate_half, ((0, 0), (0, 128 - TOPK)))], axis=1
        )
    )
    expert_back = own_back[:, :model_width]
    gate_grad = own_back[:, model_width : model_width + TOPK]
    block_rows = (hidden + residual_scale * narrow(out_home)).astype(jnp.bfloat16)

    def send_home(index):
        stacked = jnp.stack([grads[h][index] for h in range(holders)])
        moved = lax.all_to_all(stacked[None], "dp", split_axis=2, concat_axis=0, tiled=True)
        return jnp.sum(
            moved.astype(jnp.float32).reshape(
                replicas, clusters * holders, moved.shape[2], half_ff
            ),
            axis=0,
        )

    own_routes = lax.dynamic_slice_in_dim(routes, own_row, local_rows, 0)
    picked_own, _, gates_dense = gate_of(normed_second, own_routes)
    gates_own = jnp.sum(jnp.where(picked_own, gates_dense[:, None, :], 0.0), axis=2)
    chosen_grad = gates_own * (gate_grad - jnp.sum(gates_own * gate_grad, axis=1, keepdims=True))
    logits_grad = jnp.sum(jnp.where(picked_own, chosen_grad[:, :, None], 0.0), axis=1)
    second_grad = expert_back + jnp.dot(logits_grad, w_router.T, precision=lax.Precision.HIGHEST)
    hidden_back, ffn_gain_grad = norm_backward(second_grad, unit_second, scale_second, ffn_gain)
    hidden_grad = out_f32 + hidden_back
    attn_grad = spread_rows((residual_scale * hidden_grad).astype(jnp.bfloat16))
    mixed_grad = jnp.dot(attn_grad, full_out, preferred_element_type=jnp.float32).astype(
        jnp.bfloat16
    )
    out_w_grad = dot_f32(attn_grad, mixed_out, ((0,), (0,)))
    dquery, key_grad, dvalues = attend_back(
        query_heads, key_heads, value_heads, allowed, log_total, mixed_grad
    )
    query_grad = (
        unrotate(dquery, cosine, sine_table)
        .astype(jnp.bfloat16)
        .reshape(row_count, heads_here * HEAD_DIM)
    )
    keys_grad = (
        unrotate(key_grad, cosine, sine_table)
        .astype(jnp.bfloat16)
        .reshape(row_count, kv_here * HEAD_DIM)
    )
    value_grad = dvalues.astype(jnp.bfloat16).reshape(row_count, kv_here * HEAD_DIM)
    qkv_grad = jnp.concatenate([query_grad, keys_grad, value_grad], axis=1)
    qkv_w_grad = dot_f32(wide_first, qkv_grad, ((0,), (0,)))
    packed_grad = scatter_weights(
        jnp.concatenate([qkv_w_grad, out_w_grad], axis=1).astype(jnp.bfloat16)
    ).astype(jnp.float32)
    first_grad = narrow(dot_f32(qkv_grad, full_qkv, ((1,), (1,))))
    tokens_back, attn_gain_grad = norm_backward(first_grad, unit_first, scale_first, attn_gain)
    tokens_grad = hidden_grad + tokens_back
    if replicas == 1:
        tall = local_rows * EXPERTS // 128
        wide = model_width // 128
        shared = share(
            jnp.concatenate(
                [
                    logits_grad.reshape(tall, 128),
                    attn_gain_grad.reshape(wide, 128),
                    ffn_gain_grad.reshape(wide, 128),
                ],
                axis=0,
            )
        )
        logits_grad_all = shared[:, :tall].reshape(rows_all.shape[0], EXPERTS)
        router_total = exact_dot(rows_all, logits_grad_all, ((0,), (0,)))
        gains = jnp.sum(shared[:, tall:], axis=0).reshape(2, model_width)
        attn_gain_total, ffn_gain_total = gains[0], gains[1]
    else:
        attn_gain_total, ffn_gain_total, router_total = lax.psum(
            (
                attn_gain_grad,
                ffn_gain_grad,
                exact_dot(normed_second, logits_grad, ((0,), (0,))),
            ),
            ("dp", "tensor"),
        )
    return (
        block_rows,
        tokens_grad,
        attn_gain_total,
        packed_grad[:, : cuts[0]],
        packed_grad[:, cuts[0] : cuts[1]],
        packed_grad[:, cuts[1] : cuts[2]],
        packed_grad[:, cuts[2] :],
        ffn_gain_total,
        router_total,
        send_home(0),
        send_home(1),
        send_home(2),
    )


def solution(mesh):
    placed = (
        P(("dp", "tensor"), None),
        P(("dp", "tensor"), None),
        P("dp", None),
        P("dp", None),
        P(),
        P("dp", "tensor"),
        P("dp", "tensor"),
        P("dp", "tensor"),
        P("dp", "tensor"),
        P(),
        P(),
        P(None, "dp", "tensor"),
        P(None, "dp", "tensor"),
        P(None, "dp", "tensor"),
    )
    return jax.shard_map(
        local,
        mesh=mesh,
        in_specs=placed,
        out_specs=(
            P(("dp", "tensor"), None),
            P(("dp", "tensor"), None),
            P(),
            P("dp", "tensor"),
            P("dp", "tensor"),
            P("dp", "tensor"),
            P("dp", "tensor"),
            P(),
            P(),
            P(None, "dp", "tensor"),
            P(None, "dp", "tensor"),
            P(None, "dp", "tensor"),
        ),
        check_vma=False,
    )
```
